32 devices in a mesh: view: 4 (over y, x), blk: 8 (over z, core).
Axes of the slice: x: 2, y: 2, z: 4, core: 2. Of those that a mesh axis runs over, the one named last changes fastest.
Arguments:
- estimate: float32 [384, 64, 256], P('blk'), may hold values from 0.5 to 2
- views_seen: float32 [4, 384, 64, 256], P('view', 'blk'), may hold values from 0.2 to 5
- weight_mask: int32 [4, 384, 64, 256], P('view', 'blk'), may hold values from 1 to 3
- psf: float32 [4, 3, 21], P('view'), may hold values from 0.05 to 1
Outputs:
- joined: float32 [384, 64, 256], P('blk')
The draws below stay inside these ranges and needn't reach their ends.
All inputs are finite; a program needn't handle non-finite values.
Results may differ from the reference program's by a relative error of at most 0.0001.
Values sent between devices are 32-bit elements; how exact they have to be, the bound alone decides.
A program may use at most 128 MiB of HBM per device.

```python
import math
import jax
import jax.numpy as jnp
from jax import lax

CY = 64
CZ = 256
TAPS = 21
ITERS = 2
VIEWS = 4
NX = 384


def plant(values, own_key, smallest, high):
    place = [jax.random.randint(jax.random.fold_in(own_key, axis), (), 0, length) for axis, length in enumerate(values.shape)]
    widest = values.shape.index(max(values.shape))
    next_to = place[:widest] + [(place[widest] + 1) % values.shape[widest]] + place[widest + 1:]
    return values.at[tuple(place)].set(smallest).at[tuple(next_to)].set(high)


def levels(rng, dims, cuts, least, top_value):
    gain = 1.0
    for dim, parts in cuts:
        heights = jax.random.uniform(jax.random.fold_in(jax.random.fold_in(rng, 6), dim), (parts,), jnp.float32, least / len(cuts), top_value / len(cuts))
        gain = gain * jnp.repeat(jnp.exp(heights), dims[dim] // parts).reshape((-1,) + (1,) * (len(dims) - 1 - dim))
    return gain


def setup_inputs(seed: int = 0) -> dict:
    seeds = jax.random.split(jax.random.key(seed), 5)
    return {
        "estimate": jnp.clip(0.5 + 1.5 * jax.random.uniform(seeds[0], (NX, CY, CZ), jnp.float32) ** levels(seeds[0], (NX, CY, CZ), ((0, 8),), -0.2, 0.2), 0.5, 2.0),
        "views_seen": jnp.clip(jnp.exp(math.log(5.0) - 3.218876 * jax.random.uniform(seeds[1], (VIEWS, NX, CY, CZ), jnp.float32) ** levels(seeds[1], (VIEWS, NX, CY, CZ), ((0, 4), (1, 8)), -0.2, 0.2)), 0.2, 5.0),
        "weight_mask": plant(jax.random.randint(seeds[2], (VIEWS, NX, CY, CZ), 1, 4), jax.random.fold_in(seeds[2], 1), 1, 3).astype(jnp.int32),
        "psf": jnp.clip(jnp.exp(math.log(1.0) - 2.9957323 * jax.random.uniform(seeds[3], (VIEWS, 3, TAPS), jnp.float32) ** levels(seeds[3], (VIEWS, 3, TAPS), ((0, 4),), -0.2, 0.2)), 0.05, 1.0),
    }


def band_matrix(kernel, out_count, in_count, offset_by):
    row_index = jnp.arange(out_count)[:, None]
    col_index = jnp.arange(in_count)[None, :]
    offset_table = col_index - row_index + offset_by
    matches = offset_table[:, :, None] == jnp.arange(kernel.shape[0])[None, None, :]
    return jnp.sum(jnp.where(matches, kernel[None, None, :], 0.0), axis=-1)


def sweep_first(padded, kernel, count):
    result = kernel[0] * padded[0:count]
    for tap in range(1, kernel.shape[0]):
        result = result + kernel[tap] * padded[tap:tap + count]
    return result


def sweep_rest(volume, kernel):
    radius = (kernel.shape[-1] - 1) // 2
    along_y = band_matrix(kernel[1], volume.shape[1], volume.shape[1], radius)
    volume = jnp.einsum('ij,xjz->xiz', along_y, volume, precision=lax.Precision.HIGHEST)
    along_z = band_matrix(kernel[2], volume.shape[2], volume.shape[2], radius)
    return jnp.einsum('xyj,kj->xyk', volume, along_z, precision=lax.Precision.HIGHEST)


def blur_volume(volume, kernel):
    radius = (kernel.shape[-1] - 1) // 2
    padded = jnp.pad(volume, ((radius, radius), (0, 0), (0, 0)))
    return sweep_rest(sweep_first(padded, kernel[0], volume.shape[0]), kernel)


def reference(estimate, views_seen, weight_mask, psf):
    normed = psf / jnp.sum(psf, axis=-1, keepdims=True)
    flipped = normed[:, :, ::-1]
    weights_all = jnp.sum(weight_mask.astype(jnp.float32), axis=0)
    for iteration in range(ITERS):
        current = estimate

        def add_view(running, pieces):
            observed, view_mask, forward, backward = pieces
            blurred = blur_volume(current, forward)
            correction = blur_volume(observed / blurred, backward)
            return running + view_mask.astype(jnp.float32) * correction, None

        numerator, _ = lax.scan(add_view, jnp.zeros_like(estimate), (views_seen, weight_mask, normed, flipped))
        estimate = estimate * numerator / weights_all
    return estimate
```

```python
import functools

import jax
import jax.numpy as jnp
from jax import lax
from jax.experimental import pallas as pl
from jax.experimental.pallas import tpu as pltpu
from jax.sharding import PartitionSpec as P

ITERS = 2
MESH = pl.DeviceIdType.MESH
F32, BF16 = jnp.float32, jnp.bfloat16


def split(value):
    high = value.astype(BF16)
    return high, (value - high.astype(F32)).astype(BF16)


def band(taps, row, size, row_sign):
    rows = lax.broadcasted_iota(jnp.int32, (size, size), 0)
    cols = lax.broadcasted_iota(jnp.int32, (size, size), 1)
    count = taps.shape[1]
    offset = (cols - rows) * row_sign + (count - 1) // 2
    total = jnp.zeros((size, size), F32)
    for k in range(count):
        total = jnp.where(offset == k, taps[row, k], total)
    return split(total)


def kernel(dims, taps, est_in, seen_in, mask_in, out,
           ext, seen, mask, wf, wsum, nums, recvs, ybuf, ymats, zmats,
           load_sem, halo_send, halo_recv, rs_send, rs_recv, ag_send, ag_recv):
    views, blks, bits = dims
    slab, cy, cz = seen.shape
    count = taps.shape[1]
    rad = (count - 1) // 2
    part = slab // bits
    chunk = part // 2
    chunks = 2 * bits
    v, b = lax.axis_index("view"), lax.axis_index("blk")
    bit = [(v // 2**p) % 2 for p in range(bits)]
    partner = [v + (1 - 2 * bit[p]) * 2**p for p in range(bits)]
    left, right = (b + blks - 1) % blks, (b + 1) % blks

    loads = [
        pltpu.make_async_copy(est_in, ext.at[0, pl.ds(rad, slab)], load_sem.at[0]),
        pltpu.make_async_copy(mask_in.at[0], mask, load_sem.at[1]),
        pltpu.make_async_copy(seen_in.at[0], seen, load_sem.at[2]),
    ]
    for load in loads:
        load.start()

    barrier = pltpu.get_barrier_semaphore()
    for p in range(bits):
        pl.semaphore_signal(barrier, inc=1, device_id=(partner[p], b), device_id_type=MESH)
    for near in (left, right):
        pl.semaphore_signal(barrier, inc=1, device_id=(v, near), device_id_type=MESH)
    pl.semaphore_wait(barrier, bits + 2)

    def halo(which, side):
        start, land, near = ((slab, 0, right), (rad, rad + slab, left))[side]
        return pltpu.make_async_remote_copy(
            src_ref=ext.at[which, pl.ds(start, rad)], dst_ref=ext.at[which, pl.ds(land, rad)],
            send_sem=halo_send.at[which, side], recv_sem=halo_recv.at[which, side],
            device_id=(v, near), device_id_type=MESH)

    def halo_start(which):
        @pl.when(b < blks - 1)
        def _():
            halo(which, 0).start()

        @pl.when(b > 0)
        def _():
            halo(which, 1).start()

    def halo_wait(which):
        @pl.when(b > 0)
        def _():
            halo(which, 0).wait_recv()

        @pl.when(b == 0)
        def _():
            ext[which, pl.ds(0, rad)] = jnp.zeros((rad, cy, cz), F32)

        @pl.when(b < blks - 1)
        def _():
            halo(which, 1).wait_recv()

        @pl.when(b == blks - 1)
        def _():
            ext[which, pl.ds(rad + slab, rad)] = jnp.zeros((rad, cy, cz), F32)

    def halo_sent(which):
        @pl.when(b < blks - 1)
        def _():
            halo(which, 0).wait_send()

        @pl.when(b > 0)
        def _():
            halo(which, 1).wait_send()

    def region(p, s):
        start, length = p * part, part
        for t in range(s):
            length //= 2
            start = start + bit[(p + t) % bits] * length
        return start, length

    def rs_slot(s, p):
        length = part // 2 ** (s + 1)
        return bits * (part - part // 2**s) + p * length, length

    def rs_copy(r, s, p):
        buf = wsum if r == 0 else nums.at[r - 1]
        start, length = region(p, s)
        length //= 2
        mine = bit[(p + s) % bits]
        slot, _ = rs_slot(s, p)
        return pltpu.make_async_remote_copy(
            src_ref=buf.at[pl.ds(start + (1 - mine) * length, length)],
            dst_ref=recvs.at[r, pl.ds(slot, length)],
            send_sem=rs_send.at[r, s, p], recv_sem=rs_recv.at[r, s, p],
            device_id=(partner[(p + s) % bits], b), device_id_type=MESH)

    def rs_take(r, s, p):
        buf = wsum if r == 0 else nums.at[r - 1]
        rs_copy(r, s, p).wait_recv()
        start, length = region(p, s + 1)
        slot, _ = rs_slot(s, p)

        def add(i, carry):
            buf[start + i] = buf[start + i] + recvs[r, slot + i]
            return carry

        lax.fori_loop(0, length, add, 0)

    def ag_copy(r, s, p):
        start, length = region(p, s + 1)
        if r < ITERS - 1:
            ref = ext.at[2 * (r + 1), pl.ds(start + rad, length)]
        else:
            ref = out.at[pl.ds(start, length)]
        return pltpu.make_async_remote_copy(
            src_ref=ref, dst_ref=ref,
            send_sem=ag_send.at[r, s, p], recv_sem=ag_recv.at[r, s, p],
            device_id=(partner[(p + s) % bits], b), device_id_type=MESH)

    def blur(which, c, back):
        first = c * chunk

        def pair(j, carry):
            base = first + 2 * j
            one = two = None
            for k in range(count + 1):
                plane = ext[which, base + k]
                if k < count:
                    term = taps[0, count - 1 - k if back else k] * plane
                    one = term if one is None else one + term
                if k > 0:
                    term = taps[0, count - k if back else k - 1] * plane
                    two = term if two is None else two + term
            for half, plane in enumerate((one, two)):
                high, low = split(plane)
                stack = jnp.concatenate([high, high, low], axis=0)
                ybuf[pl.ds((2 * j + half) * cy, cy)] = jnp.dot(
                    ymats[back], stack, preferred_element_type=F32)
            return carry

        lax.fori_loop(0, chunk // 2, pair, 0)
        high, low = split(ybuf[...])
        high_mat, low_mat = zmats[back, 0], zmats[back, 1]
        result = jnp.dot(high, high_mat, preferred_element_type=F32)
        result += jnp.dot(low, high_mat, preferred_element_type=F32)
        result += jnp.dot(high, low_mat, preferred_element_type=F32)
        return result.reshape(chunk, cy, cz)

    inner = [c for c in range(chunks) if c * chunk >= rad and (c + 1) * chunk <= slab - rad]
    low_c, high_c = (inner[0], inner[-1] + 1) if inner else (0, 0)

    def over_inner(step):
        if inner:
            def run(c, carry):
                step(c)
                return carry

            lax.fori_loop(low_c, high_c, run, 0)

    def over_edges(step):
        def run(t, carry):
            step(t + (t // max(low_c, 1)) * (high_c - low_c) if 2 * low_c == chunks - (high_c - low_c) else t)
            return carry

        lax.fori_loop(0, chunks - (high_c - low_c), run, 0)

    loads[0].wait()
    halo_start(0)
    loads[1].wait()

    def to_float(i, carry):
        weights = mask[i].astype(F32)
        wf[i] = weights
        wsum[i] = weights
        return carry

    lax.fori_loop(0, slab, to_float, 0)
    for p in range(bits):
        rs_copy(0, 0, p).start()

    for back in range(2):
        sign = -1 if back else 1
        high, low = band(taps, 1, cy, sign)
        ymats[back] = jnp.concatenate([high, low, high], axis=1)
        high, low = band(taps, 2, cz, -sign)
        zmats[back, 0] = high
        zmats[back, 1] = low
    loads[2].wait()

    for r in range(ITERS):
        here, there = 2 * r, 2 * r + 1

        def quotient(c):
            blurred = blur(here, c, 0)
            rows = pl.ds(c * chunk, chunk)
            ext[there, pl.ds(rad + c * chunk, chunk)] = seen[rows] / blurred

        over_inner(quotient)
        halo_wait(here)
        over_edges(quotient)
        halo_start(there)
        if r == 0:
            for p in range(bits):
                rs_take(0, 0, p)
                if bits > 1:
                    rs_copy(0, 1, p).start()

        def correct(c):
            corrected = blur(there, c, 1)
            rows = pl.ds(c * chunk, chunk)
            nums[r, rows] = wf[rows] * corrected
            for p in range(bits):
                @pl.when(c == 2 * p + 1 - bit[p])
                def _(p=p):
                    rs_copy(r + 1, 0, p).start()

        over_inner(correct)
        halo_wait(there)
        over_edges(correct)
        if r == 0:
            for s in range(1, bits):
                for p in range(bits):
                    rs_take(0, s, p)
                    if s + 1 < bits:
                        rs_copy(0, s + 1, p).start()
        for s in range(bits):
            for p in range(bits):
                rs_take(r + 1, s, p)
                if s + 1 < bits:
                    rs_copy(r + 1, s + 1, p).start()
                else:
                    start, length = region(p, bits)

                    def update(i, carry):
                        cell = start + i
                        fresh = ext[here, rad + cell] * nums[r, cell] / wsum[cell]
                        if r < ITERS - 1:
                            ext[here + 2, rad + cell] = fresh
                        else:
                            out[cell] = fresh
                        return carry

                    lax.fori_loop(0, length, update, 0)
                    ag_copy(r, s, p).start()
        for s in range(bits - 1, -1, -1):
            for p in range(bits):
                ag_copy(r, s, p).wait_recv()
                if s > 0:
                    ag_copy(r, s - 1, p).start()
        if r < ITERS - 1:
            halo_start(here + 2)

    for which in range(2 * ITERS):
        halo_sent(which)
    for s in range(bits):
        for p in range(bits):
            for r in range(ITERS + 1):
                rs_copy(r, s, p).wait_send()
            for r in range(ITERS):
                ag_copy(r, s, p).wait_send()


def body(views, blks, estimate, views_seen, weight_mask, psf):
    slab, cy, cz = estimate.shape
    bits = views.bit_length() - 1
    count = psf.shape[-1]
    rad = (count - 1) // 2
    chunk = slab // bits // 2
    taps = (psf / jnp.sum(psf, axis=-1, keepdims=True))[0]
    hbm = pl.BlockSpec(memory_space=pl.ANY)
    vmem = pltpu.VMEM
    dma = pltpu.SemaphoreType.DMA
    landing = bits * (slab // bits - slab // bits // views)
    return pl.pallas_call(
        functools.partial(kernel, (views, blks, bits)),
        out_shape=jax.ShapeDtypeStruct(estimate.shape, F32),
        in_specs=[pl.BlockSpec(memory_space=pltpu.SMEM), hbm, hbm, hbm],
        out_specs=pl.BlockSpec(memory_space=pltpu.VMEM),
        scratch_shapes=[
            vmem((2 * ITERS, slab + 2 * rad, cy, cz), F32),
            vmem((slab, cy, cz), F32),
            vmem((slab, cy, cz), jnp.int32),
            vmem((slab, cy, cz), F32),
            vmem((slab, cy, cz), F32),
            vmem((ITERS, slab, cy, cz), F32),
            vmem((ITERS + 1, landing, cy, cz), F32),
            vmem((chunk * cy, cz), F32),
            vmem((2, cy, 3 * cy), BF16),
            vmem((2, 2, cz, cz), BF16),
            dma((3,)),
            dma((2 * ITERS, 2)),
            dma((2 * ITERS, 2)),
            dma((ITERS + 1, bits, bits)),
            dma((ITERS + 1, bits, bits)),
            dma((ITERS, bits, bits)),
            dma((ITERS, bits, bits)),
        ],
        compiler_params=pltpu.CompilerParams(
            collective_id=0, has_side_effects=True, vmem_limit_bytes=60 * 2**20),
    )(taps, estimate, views_seen, weight_mask)


def solution(mesh):
    placed = (
        P("blk", None, None),
        P("view", "blk", None, None),
        P("view", "blk", None, None),
        P("view", None, None),
    )
    return jax.shard_map(
        functools.partial(body, mesh.shape["view"], mesh.shape["blk"]),
        mesh=mesh, in_specs=placed, out_specs=P("blk", None, None), check_vma=False
    )
```

```python
import functools

import jax
import jax.numpy as jnp
from jax import lax
from jax.experimental import pallas as pl
from jax.experimental.pallas import tpu as pltpu
from jax.sharding import PartitionSpec as P

ITERS = 2
MESH = pl.DeviceIdType.MESH
F32, BF16 = jnp.float32, jnp.bfloat16


def split(value):
    high = value.astype(BF16)
    return high, (value - high.astype(F32)).astype(BF16)


def band(taps, row, size, row_sign, scale):
    rows = lax.broadcasted_iota(jnp.int32, (size, size), 0)
    cols = lax.broadcasted_iota(jnp.int32, (size, size), 1)
    count = taps.shape[2]
    offset = (cols - rows) * row_sign + (count - 1) // 2
    total = jnp.zeros((size, size), F32)
    for k in range(count):
        total = jnp.where(offset == k, taps[0, row, k], total)
    return split(total * scale)


def kernel(dims, taps, est_in, seen_in, mask_in, out, final,
           ext, seen, mask, wf, wsum, nums, recvs, ybuf, ymats, zmats,
           load_sem, store_sem, halo_send, halo_recv, rs_send, rs_recv, ag_send, ag_recv):
    views, blks, bits = dims
    slab, cy, cz = seen.shape
    count = taps.shape[2]
    rad = (count - 1) // 2
    chunks = 2 * bits
    chunk = slab // chunks
    inner = [c for c in range(chunks) if c * chunk >= rad and (c + 1) * chunk <= slab - rad]
    edges = [c for c in range(chunks) if c not in inner]
    order = edges + inner
    turn = [order.index(c) % bits for c in range(chunks)]
    v, b = lax.axis_index("view"), lax.axis_index("blk")
    bit = [(v // 2**p) % 2 for p in range(bits)]
    partner = [v + (1 - 2 * bit[p]) * 2**p for p in range(bits)]
    left, right = (b + blks - 1) % blks, (b + 1) % blks

    loads = [
        pltpu.make_async_copy(est_in, ext.at[0, pl.ds(rad, slab)], load_sem.at[0]),
        pltpu.make_async_copy(mask_in.at[0], mask, load_sem.at[1]),
        pltpu.make_async_copy(seen_in.at[0], seen, load_sem.at[2]),
    ]
    for load in loads:
        load.start()

    barrier = pltpu.get_barrier_semaphore()
    for p in range(bits):
        pl.semaphore_signal(barrier, inc=1, device_id=(partner[p], b), device_id_type=MESH)
    for near in (left, right):
        pl.semaphore_signal(barrier, inc=1, device_id=(v, near), device_id_type=MESH)
    pl.semaphore_wait(barrier, bits + 2)

    def halo(which, side):
        start, land, near = ((slab, 0, right), (rad, rad + slab, left))[side]
        return pltpu.make_async_remote_copy(
            src_ref=ext.at[which, pl.ds(start, rad)], dst_ref=ext.at[which, pl.ds(land, rad)],
            send_sem=halo_send.at[which, side], recv_sem=halo_recv.at[which, side],
            device_id=(v, near), device_id_type=MESH)

    def halo_start(which):
        @pl.when(b < blks - 1)
        def _():
            halo(which, 0).start()

        @pl.when(b > 0)
        def _():
            halo(which, 1).start()

    def halo_wait(which):
        @pl.when(b > 0)
        def _():
            halo(which, 0).wait_recv()

        @pl.when(b == 0)
        def _():
            ext[which, pl.ds(0, rad)] = jnp.zeros((rad, cy, cz), F32)

        @pl.when(b < blks - 1)
        def _():
            halo(which, 1).wait_recv()

        @pl.when(b == blks - 1)
        def _():
            ext[which, pl.ds(rad + slab, rad)] = jnp.zeros((rad, cy, cz), F32)

    def halo_sent(which):
        @pl.when(b < blks - 1)
        def _():
            halo(which, 0).wait_send()

        @pl.when(b > 0)
        def _():
            halo(which, 1).wait_send()

    def way(p, s):
        return (turn[p] + s) % bits

    def region(p, s):
        start, length = p * chunk, chunk
        for t in range(s):
            length //= 2
            start = start + bit[way(p, t)] * length
        return start, length

    def rs_slot(s, p):
        length = chunk // 2 ** (s + 1)
        return chunks * (chunk - chunk // 2**s) + p * length, length

    def rs_copy(r, s, p):
        buf = wsum if r == 0 else nums.at[r - 1]
        start, length = region(p, s)
        length //= 2
        mine = bit[way(p, s)]
        slot, _ = rs_slot(s, p)
        return pltpu.make_async_remote_copy(
            src_ref=buf.at[pl.ds(start + (1 - mine) * length, length)],
            dst_ref=recvs.at[r, pl.ds(slot, length)],
            send_sem=rs_send.at[r, s, p], recv_sem=rs_recv.at[r, s, p],
            device_id=(partner[way(p, s)], b), device_id_type=MESH)

    def rs_take(r, s, p):
        buf = wsum if r == 0 else nums.at[r - 1]
        rs_copy(r, s, p).wait_recv()
        start, length = region(p, s + 1)
        slot, _ = rs_slot(s, p)

        def add(i, carry):
            buf[start + i] = buf[start + i] + recvs[r, slot + i]
            return carry

        lax.fori_loop(0, length, add, 0)

    def ag_copy(r, s, p):
        start, length = region(p, s + 1)
        if r < ITERS - 1:
            ref = ext.at[2 * (r + 1), pl.ds(start + rad, length)]
        else:
            ref = final.at[pl.ds(start, length)]
        return pltpu.make_async_remote_copy(
            src_ref=ref, dst_ref=ref,
            send_sem=ag_send.at[r, s, p], recv_sem=ag_recv.at[r, s, p],
            device_id=(partner[way(p, s)], b), device_id_type=MESH)

    def store(p):
        rows = pl.ds(p * chunk, chunk)
        return pltpu.make_async_copy(final.at[rows], out.at[rows], store_sem.at[p])

    def blur(which, c, back):
        first = c * chunk

        def pair(j, carry):
            base = first + 2 * j
            one = two = None
            for k in range(count + 1):
                plane = ext[which, base + k]
                if k < count:
                    term = taps[0, 0, count - 1 - k if back else k] * plane
                    one = term if one is None else one + term
                if k > 0:
                    term = taps[0, 0, count - k if back else k - 1] * plane
                    two = term if two is None else two + term
            for half, plane in enumerate((one, two)):
                high, low = split(plane)
                stack = jnp.concatenate([high, high, low], axis=0)
                ybuf[pl.ds((2 * j + half) * cy, cy)] = jnp.dot(
                    ymats[back], stack, preferred_element_type=F32)
            return carry

        lax.fori_loop(0, chunk // 2, pair, 0)
        high, low = split(ybuf[...])
        high_mat, low_mat = zmats[back, 0], zmats[back, 1]
        result = jnp.dot(high, high_mat, preferred_element_type=F32)
        result += jnp.dot(low, high_mat, preferred_element_type=F32)
        result += jnp.dot(high, low_mat, preferred_element_type=F32)
        return result.reshape(chunk, cy, cz)

    low_c = inner[0] if inner else 0
    gap = len(inner)

    def over_inner(step):
        def run(c, carry):
            step(c)
            return carry

        if inner:
            lax.fori_loop(low_c, low_c + gap, run, 0)

    def over_edges(step):
        def run(t, carry):
            step(t + (t // low_c) * gap if inner else t)
            return carry

        lax.fori_loop(0, len(edges), run, 0)

    loads[0].wait()
    halo_start(0)
    loads[1].wait()

    def to_float(i, carry):
        weights = mask[i].astype(F32)
        wf[i] = weights
        wsum[i] = weights
        return carry

    lax.fori_loop(0, slab, to_float, 0)
    for p in order:
        rs_copy(0, 0, p).start()

    sums = []
    for row in range(3):
        total = taps[0, row, 0]
        for k in range(1, count):
            total = total + taps[0, row, k]
        sums.append(jnp.full((1, cz), total, F32))
    y_scale = (1.0 / (sums[0] * sums[1]))[:, :cy]
    z_scale = 1.0 / sums[2]
    for back in range(2):
        sign = -1 if back else 1
        high, low = band(taps, 1, cy, sign, y_scale)
        ymats[back] = jnp.concatenate([high, low, high], axis=1)
        high, low = band(taps, 2, cz, -sign, z_scale)
        zmats[back, 0] = high
        zmats[back, 1] = low
    loads[2].wait()

    for r in range(ITERS):
        here, there = 2 * r, 2 * r + 1

        def quotient(c):
            blurred = blur(here, c, 0)
            rows = pl.ds(c * chunk, chunk)
            ext[there, pl.ds(rad + c * chunk, chunk)] = seen[rows] / blurred

        halo_wait(here)
        over_edges(quotient)
        halo_start(there)
        over_inner(quotient)
        if r == 0:
            for p in order:
                rs_take(0, 0, p)
                if bits > 1:
                    rs_copy(0, 1, p).start()

        def correct(c):
            corrected = blur(there, c, 1)
            rows = pl.ds(c * chunk, chunk)
            nums[r, rows] = wf[rows] * corrected
            for p in range(chunks):
                @pl.when(c == p)
                def _(p=p):
                    rs_copy(r + 1, 0, p).start()

        halo_wait(there)
        over_edges(correct)
        over_inner(correct)
        if r == 0:
            for s in range(1, bits):
                for p in order:
                    rs_take(0, s, p)
                    if s + 1 < bits:
                        rs_copy(0, s + 1, p).start()

        def update(p):
            start, length = region(p, bits)

            def cells(i, carry):
                cell = start + i
                fresh = ext[here, rad + cell] * nums[r, cell] / wsum[cell]
                if r < ITERS - 1:
                    ext[here + 2, rad + cell] = fresh
                else:
                    final[cell] = fresh
                return carry

            lax.fori_loop(0, length, cells, 0)

        events = [(e, pos) for e in range(2 * bits) for pos in range(chunks)]
        events.sort(key=lambda ev: (ev[0] + ev[1] // bits, -(ev[1] // bits), ev[1] % bits))
        arrived = set()
        for e, pos in events:
            p = order[pos]
            if e < bits:
                rs_take(r + 1, e, p)
                if e + 1 < bits:
                    rs_copy(r + 1, e + 1, p).start()
                else:
                    update(p)
                    ag_copy(r, bits - 1, p).start()
            else:
                s = 2 * bits - 1 - e
                ag_copy(r, s, p).wait_recv()
                if s > 0:
                    ag_copy(r, s - 1, p).start()
                elif r < ITERS - 1:
                    if not set(edges) <= arrived and set(edges) <= arrived | {p}:
                        halo_start(here + 2)
                    arrived.add(p)
                else:
                    store(p).start()

    for p in range(chunks):
        store(p).wait()
    for which in range(2 * ITERS):
        halo_sent(which)
    for s in range(bits):
        for p in range(chunks):
            for r in range(ITERS + 1):
                rs_copy(r, s, p).wait_send()
            for r in range(ITERS):
                ag_copy(r, s, p).wait_send()


def body(views, blks, estimate, views_seen, weight_mask, psf):
    slab, cy, cz = estimate.shape
    bits = views.bit_length() - 1
    count = psf.shape[-1]
    rad = (count - 1) // 2
    chunk = slab // (2 * bits)
    hbm = pl.BlockSpec(memory_space=pl.ANY)
    vmem = pltpu.VMEM
    dma = pltpu.SemaphoreType.DMA
    landing = slab - slab // views
    chunks = 2 * bits
    return pl.pallas_call(
        functools.partial(kernel, (views, blks, bits)),
        out_shape=jax.ShapeDtypeStruct(estimate.shape, F32),
        in_specs=[pl.BlockSpec(memory_space=pltpu.SMEM), hbm, hbm, hbm],
        out_specs=hbm,
        scratch_shapes=[
            vmem((slab, cy, cz), F32),
            vmem((2 * ITERS, slab + 2 * rad, cy, cz), F32),
            vmem((slab, cy, cz), F32),
            vmem((slab, cy, cz), jnp.int32),
            vmem((slab, cy, cz), F32),
            vmem((slab, cy, cz), F32),
            vmem((ITERS, slab, cy, cz), F32),
            vmem((ITERS + 1, landing, cy, cz), F32),
            vmem((chunk * cy, cz), F32),
            vmem((2, cy, 3 * cy), BF16),
            vmem((2, 2, cz, cz), BF16),
            dma((3,)),
            dma((chunks,)),
            dma((2 * ITERS, 2)),
            dma((2 * ITERS, 2)),
            dma((ITERS + 1, bits, chunks)),
            dma((ITERS + 1, bits, chunks)),
            dma((ITERS, bits, chunks)),
            dma((ITERS, bits, chunks)),
        ],
        compiler_params=pltpu.CompilerParams(
            collective_id=0, has_side_effects=True, vmem_limit_bytes=60 * 2**20),
    )(psf, estimate, views_seen, weight_mask)


def solution(mesh):
    placed = (
        P("blk", None, None),
        P("view", "blk", None, None),
        P("view", "blk", None, None),
        P("view", None, None),
    )
    return jax.shard_map(
        functools.partial(body, mesh.shape["view"], mesh.shape["blk"]),
        mesh=mesh, in_specs=placed, out_specs=P("blk", None, None), check_vma=False
    )
```

```python
import functools

import jax
import jax.numpy as jnp
from jax import lax
from jax.experimental import pallas as pl
from jax.experimental.pallas import tpu as pltpu
from jax.sharding import PartitionSpec as P

ITERS = 2
MESH = pl.DeviceIdType.MESH
F32, BF16 = jnp.float32, jnp.bfloat16


def split(value):
    high = value.astype(BF16)
    return high, (value - high.astype(F32)).astype(BF16)


def band(taps, row, size, row_sign, scale):
    rows = lax.broadcasted_iota(jnp.int32, (size, size), 0)
    cols = lax.broadcasted_iota(jnp.int32, (size, size), 1)
    count = taps.shape[2]
    offset = (cols - rows) * row_sign + (count - 1) // 2
    total = jnp.zeros((size, size), F32)
    for k in range(count):
        total = jnp.where(offset == k, taps[0, row, k], total)
    return split(total * scale)


def kernel(dims, taps, est_in, seen_in, mask_in, out, final,
           ext, seen, mask, wf, wsum, nums, recvs, xbuf, ymats, zmats,
           load_sem, store_sem, halo_send, halo_recv, rs_send, rs_recv, ag_send, ag_recv):
    views, blks, bits = dims
    slab, cy, cz = seen.shape
    count = taps.shape[2]
    rad = (count - 1) // 2
    chunks = 2 * bits
    chunk = slab // chunks
    inner = [c for c in range(chunks) if c * chunk >= rad and (c + 1) * chunk <= slab - rad]
    edges = [c for c in range(chunks) if c not in inner]
    order = edges + inner
    turn = [order.index(c) % bits for c in range(chunks)]
    v, b = lax.axis_index("view"), lax.axis_index("blk")
    bit = [(v // 2**p) % 2 for p in range(bits)]
    partner = [v + (1 - 2 * bit[p]) * 2**p for p in range(bits)]
    left, right = (b + blks - 1) % blks, (b + 1) % blks

    loads = [
        pltpu.make_async_copy(est_in, ext.at[0, pl.ds(rad, slab)], load_sem.at[0]),
        pltpu.make_async_copy(mask_in.at[0], mask, load_sem.at[1]),
        pltpu.make_async_copy(seen_in.at[0], seen, load_sem.at[2]),
    ]
    for load in loads:
        load.start()

    barrier = pltpu.get_barrier_semaphore()
    for p in range(bits):
        pl.semaphore_signal(barrier, inc=1, device_id=(partner[p], b), device_id_type=MESH)
    for near in (left, right):
        pl.semaphore_signal(barrier, inc=1, device_id=(v, near), device_id_type=MESH)
    pl.semaphore_wait(barrier, bits + 2)

    def halo(which, side):
        start, land, near = ((slab, 0, right), (rad, rad + slab, left))[side]
        return pltpu.make_async_remote_copy(
            src_ref=ext.at[which, pl.ds(start, rad)], dst_ref=ext.at[which, pl.ds(land, rad)],
            send_sem=halo_send.at[which, side], recv_sem=halo_recv.at[which, side],
            device_id=(v, near), device_id_type=MESH)

    def halo_start(which):
        @pl.when(b < blks - 1)
        def _():
            halo(which, 0).start()

        @pl.when(b > 0)
        def _():
            halo(which, 1).start()

    def halo_wait(which):
        @pl.when(b > 0)
        def _():
            halo(which, 0).wait_recv()

        @pl.when(b == 0)
        def _():
            ext[which, pl.ds(0, rad)] = jnp.zeros((rad, cy, cz), F32)

        @pl.when(b < blks - 1)
        def _():
            halo(which, 1).wait_recv()

        @pl.when(b == blks - 1)
        def _():
            ext[which, pl.ds(rad + slab, rad)] = jnp.zeros((rad, cy, cz), F32)

    def halo_sent(which):
        @pl.when(b < blks - 1)
        def _():
            halo(which, 0).wait_send()

        @pl.when(b > 0)
        def _():
            halo(which, 1).wait_send()

    def way(p, s):
        return (turn[p] + s) % bits

    def region(p, s):
        start, length = p * chunk, chunk
        for t in range(s):
            length //= 2
            start = start + bit[way(p, t)] * length
        return start, length

    def rs_slot(s, p):
        length = chunk // 2 ** (s + 1)
        return chunks * (chunk - chunk // 2**s) + p * length, length

    def rs_copy(r, s, p):
        buf = wsum if r == 0 else nums.at[r - 1]
        start, length = region(p, s)
        length //= 2
        mine = bit[way(p, s)]
        slot, _ = rs_slot(s, p)
        return pltpu.make_async_remote_copy(
            src_ref=buf.at[pl.ds(start + (1 - mine) * length, length)],
            dst_ref=recvs.at[r, pl.ds(slot, length)],
            send_sem=rs_send.at[r, s, p], recv_sem=rs_recv.at[r, s, p],
            device_id=(partner[way(p, s)], b), device_id_type=MESH)

    def rs_take(r, s, p):
        buf = wsum if r == 0 else nums.at[r - 1]
        rs_copy(r, s, p).wait_recv()
        start, length = region(p, s + 1)
        slot, _ = rs_slot(s, p)

        def add(i, carry):
            buf[start + i] = buf[start + i] + recvs[r, slot + i]
            return carry

        lax.fori_loop(0, length, add, 0)

    def ag_copy(r, s, p):
        start, length = region(p, s + 1)
        if r < ITERS - 1:
            ref = ext.at[2 * (r + 1), pl.ds(start + rad, length)]
        else:
            ref = final.at[pl.ds(start, length)]
        return pltpu.make_async_remote_copy(
            src_ref=ref, dst_ref=ref,
            send_sem=ag_send.at[r, s, p], recv_sem=ag_recv.at[r, s, p],
            device_id=(partner[way(p, s)], b), device_id_type=MESH)

    def store(p):
        rows = pl.ds(p * chunk, chunk)
        return pltpu.make_async_copy(final.at[rows], out.at[rows], store_sem.at[p])

    def blur(which, c, back):
        first = c * chunk

        height, lanes = 8, 256

        def block(j, carry):
            line = pl.multiple_of((j // (cz // lanes)) * height, height)
            column = pl.multiple_of((j % (cz // lanes)) * lanes, lanes)
            window = (pl.ds(line, height), pl.ds(column, lanes))
            totals = [None] * chunk
            for k in range(count + chunk - 1):
                plane = ext[(which, first + k) + window]
                for i in range(max(0, k - count + 1), min(chunk, k + 1)):
                    tap = k - i
                    term = taps[0, 0, count - 1 - tap if back else tap] * plane
                    totals[i] = term if totals[i] is None else totals[i] + term
            for i in range(chunk):
                xbuf[(i,) + window] = totals[i]
            return carry

        lax.fori_loop(0, (cy // height) * (cz // lanes), block, 0)
        blurred = []
        for i in range(chunk):
            high, low = split(xbuf[i])
            stack = jnp.concatenate([high, high, low], axis=0)
            blurred.append(jnp.dot(ymats[back], stack, preferred_element_type=F32))
        high, low = split(jnp.concatenate(blurred, axis=0))
        high_mat, low_mat = zmats[back, 0], zmats[back, 1]
        result = jnp.dot(high, high_mat, preferred_element_type=F32)
        result += jnp.dot(low, high_mat, preferred_element_type=F32)
        result += jnp.dot(high, low_mat, preferred_element_type=F32)
        return result.reshape(chunk, cy, cz)

    low_c = inner[0] if inner else 0
    gap = len(inner)

    def over_inner(step):
        def run(c, carry):
            step(c)
            return carry

        if inner:
            lax.fori_loop(low_c, low_c + gap, run, 0)

    def over_edges(step):
        def run(t, carry):
            step(t + (t // low_c) * gap if inner else t)
            return carry

        lax.fori_loop(0, len(edges), run, 0)

    loads[0].wait()
    halo_start(0)
    loads[1].wait()

    def to_float(i, carry):
        weights = mask[i].astype(F32)
        wf[i] = weights
        wsum[i] = weights
        return carry

    lax.fori_loop(0, slab, to_float, 0)
    for p in order:
        rs_copy(0, 0, p).start()

    sums = []
    for row in range(3):
        total = taps[0, row, 0]
        for k in range(1, count):
            total = total + taps[0, row, k]
        sums.append(jnp.full((1, cz), total, F32))
    y_scale = (1.0 / (sums[0] * sums[1]))[:, :cy]
    z_scale = 1.0 / sums[2]
    for back in range(2):
        sign = -1 if back else 1
        high, low = band(taps, 1, cy, sign, y_scale)
        ymats[back] = jnp.concatenate([high, low, high], axis=1)
        high, low = band(taps, 2, cz, -sign, z_scale)
        zmats[back, 0] = high
        zmats[back, 1] = low
    loads[2].wait()

    for r in range(ITERS):
        here, there = 2 * r, 2 * r + 1

        def quotient(c):
            blurred = blur(here, c, 0)
            rows = pl.ds(c * chunk, chunk)
            ext[there, pl.ds(rad + c * chunk, chunk)] = seen[rows] / blurred

        halo_wait(here)
        over_edges(quotient)
        halo_start(there)
        over_inner(quotient)
        if r == 0:
            for p in order:
                rs_take(0, 0, p)
                if bits > 1:
                    rs_copy(0, 1, p).start()

        def correct(c):
            corrected = blur(there, c, 1)
            rows = pl.ds(c * chunk, chunk)
            nums[r, rows] = wf[rows] * corrected
            for p in range(chunks):
                @pl.when(c == p)
                def _(p=p):
                    rs_copy(r + 1, 0, p).start()

        halo_wait(there)
        over_edges(correct)
        over_inner(correct)
        if r == 0:
            for s in range(1, bits):
                for p in order:
                    rs_take(0, s, p)
                    if s + 1 < bits:
                        rs_copy(0, s + 1, p).start()

        def update(p):
            start, length = region(p, bits)

            def cells(i, carry):
                cell = start + i
                fresh = ext[here, rad + cell] * nums[r, cell] / wsum[cell]
                if r < ITERS - 1:
                    ext[here + 2, rad + cell] = fresh
                else:
                    final[cell] = fresh
                return carry

            lax.fori_loop(0, length, cells, 0)

        events = [(e, pos) for e in range(2 * bits) for pos in range(chunks)]
        events.sort(key=lambda ev: (ev[0] + ev[1] // bits, -(ev[1] // bits), ev[1] % bits))
        arrived = set()
        for e, pos in events:
            p = order[pos]
            if e < bits:
                rs_take(r + 1, e, p)
                if e + 1 < bits:
                    rs_copy(r + 1, e + 1, p).start()
                else:
                    update(p)
                    ag_copy(r, bits - 1, p).start()
            else:
                s = 2 * bits - 1 - e
                ag_copy(r, s, p).wait_recv()
                if s > 0:
                    ag_copy(r, s - 1, p).start()
                elif r < ITERS - 1:
                    if not set(edges) <= arrived and set(edges) <= arrived | {p}:
                        halo_start(here + 2)
                    arrived.add(p)
                else:
                    store(p).start()

    for p in range(chunks):
        store(p).wait()
    for which in range(2 * ITERS):
        halo_sent(which)
    for s in range(bits):
        for p in range(chunks):
            for r in range(ITERS + 1):
                rs_copy(r, s, p).wait_send()
            for r in range(ITERS):
                ag_copy(r, s, p).wait_send()


def body(views, blks, estimate, views_seen, weight_mask, psf):
    slab, cy, cz = estimate.shape
    bits = views.bit_length() - 1
    count = psf.shape[-1]
    rad = (count - 1) // 2
    chunk = slab // (2 * bits)
    hbm = pl.BlockSpec(memory_space=pl.ANY)
    vmem = pltpu.VMEM
    dma = pltpu.SemaphoreType.DMA
    landing = slab - slab // views
    chunks = 2 * bits
    return pl.pallas_call(
        functools.partial(kernel, (views, blks, bits)),
        out_shape=jax.ShapeDtypeStruct(estimate.shape, F32),
        in_specs=[pl.BlockSpec(memory_space=pltpu.SMEM), hbm, hbm, hbm],
        out_specs=hbm,
        scratch_shapes=[
            vmem((slab, cy, cz), F32),
            vmem((2 * ITERS, slab + 2 * rad, cy, cz), F32),
            vmem((slab, cy, cz), F32),
            vmem((slab, cy, cz), jnp.int32),
            vmem((slab, cy, cz), F32),
            vmem((slab, cy, cz), F32),
            vmem((ITERS, slab, cy, cz), F32),
            vmem((ITERS + 1, landing, cy, cz), F32),
            vmem((chunk, cy, cz), F32),
            vmem((2, cy, 3 * cy), BF16),
            vmem((2, 2, cz, cz), BF16),
            dma((3,)),
            dma((chunks,)),
            dma((2 * ITERS, 2)),
            dma((2 * ITERS, 2)),
            dma((ITERS + 1, bits, chunks)),
            dma((ITERS + 1, bits, chunks)),
            dma((ITERS, bits, chunks)),
            dma((ITERS, bits, chunks)),
        ],
        compiler_params=pltpu.CompilerParams(
            collective_id=0, has_side_effects=True, vmem_limit_bytes=60 * 2**20),
    )(psf, estimate, views_seen, weight_mask)


def solution(mesh):
    placed = (
        P("blk", None, None),
        P("view", "blk", None, None),
        P("view", "blk", None, None),
        P("view", None, None),
    )
    return jax.shard_map(
        functools.partial(body, mesh.shape["view"], mesh.shape["blk"]),
        mesh=mesh, in_specs=placed, out_specs=P("blk", None, None), check_vma=False
    )
```
